32 devices in a mesh: view: 2 (over x), tm: 16 (over z, y, core).
Axes of the slice: x: 2, y: 2, z: 4, core: 2. Of those that a mesh axis runs over, the one named last changes fastest.
Arguments:
- hidden_in: bfloat16 [2, 4096, 1024], P('view', 'tm'), may hold values from -8 to 8
- ssm_input: bfloat16 [2, 4096, 1024], P('view', 'tm'), may hold values from -6 to 6
- gate_input: bfloat16 [2, 4096, 1024], P('view', 'tm'), may hold values from -6 to 6
- write_map: bfloat16 [2, 4096, 128], P('view', 'tm'), may hold values from -6 to 6
- read_map: bfloat16 [2, 4096, 128], P('view', 'tm'), may hold values from -6 to 6
- step_size: float32 [2, 4096, 16], P('view', 'tm'), may hold values from 0 to 1, as said below
- decay_log: float32 [16], replicated, may hold values from 0 to 2
- skip_gain: float32 [16], replicated, may hold values from 0.5 to 1.5
- norm_gain: float32 [1024], replicated, may hold values from 0.25 to 1.75
- mixer_out: bfloat16 [1024, 1024], P(('view', 'tm')), may hold values from -0.1875 to 0.1875
- attn_gain: float32 [1024], replicated, may hold values from 0.25 to 1.75
- head_proj: bfloat16 [1024, 1536], P(None, 'view'), may hold values from -8 to 8
- attn_out: bfloat16 [512, 1024], P(None, ('view', 'tm')), may hold values from -0.25 to 0.25
Outputs:
- output: bfloat16 [2, 4096, 1024], P('view', 'tm')
The draws below stay inside these ranges and needn't reach their ends.
Inputs may be any that keep to these rules, and one draw needn't show every extreme that they name: `step_size`: positive.
All inputs are finite; a program needn't handle non-finite values.
Results may differ from the reference program's by a relative error of at most 0.0063.
Values may be sent and summed in bfloat16 or wider, within the bound.
No kernel may reach another device: no remote copies, remote signals or barrier semaphores. Data moves between devices by JAX's collectives and lax.ppermute only.
A program may use at most 128 MiB of HBM per device.

```python
import math
import jax
import jax.numpy as jnp
from jax import lax

D = 1024
HEADS = 16
HDIM = 64
STATE = 128
BLOCK = 128
AHEADS = 8
AHD = 64
INNER = 1024
VIEWS = 2
FRAME_COUNT = 4096


def rate_table(base_key):
    table_key = jax.random.fold_in(base_key, 11)
    first_key, second_key, third_key, fourth_key = jax.random.split(table_key, 4)
    slow_share = 0.6
    slow_heads = jax.random.uniform(first_key, (HEADS,)) < slow_share
    slow_rate = jnp.exp(jax.random.uniform(second_key, (HEADS,), minval=math.log(0.05 / FRAME_COUNT), maxval=math.log(1.0 / FRAME_COUNT)))
    fast_rate = jnp.exp(jax.random.uniform(third_key, (HEADS,), minval=math.log(0.02), maxval=math.log(0.035)))
    rate = jnp.where(slow_heads, slow_rate, fast_rate)
    log_magnitude = jax.random.uniform(fourth_key, (HEADS,), minval=0.0, maxval=math.log(4.0))
    return (log_magnitude, rate / jnp.exp(log_magnitude))


def draw_decay_log(key, part):
    return rate_table(key)[0].astype(jnp.float32)


def draw_step_size(key, part):
    log_magnitude, initial_step = rate_table(key)
    own_key = jax.random.fold_in(key, 23)
    rough_key, spot_key, jump_key = jax.random.split(own_key, 3)
    coarse_noise = jnp.exp(jax.random.uniform(rough_key, (VIEWS, FRAME_COUNT, HEADS), minval=math.log(0.5), maxval=math.log(2.0)))
    sample_points = jax.random.randint(spot_key, (VIEWS, 6), 0, FRAME_COUNT)
    sudden_spike = jnp.any(jnp.arange(FRAME_COUNT)[None, :, None] == sample_points[:, None, :], axis=-1)
    skip_forward = jax.random.uniform(jump_key, (VIEWS, FRAME_COUNT, HEADS), minval=0.22, maxval=0.7) / jnp.exp(log_magnitude)
    return (initial_step * coarse_noise + jnp.where(sudden_spike[:, :, None], skip_forward, 0.0)).astype(jnp.float32)


def draw_hidden_in(key, part):
    own_key = jax.random.fold_in(key, 31)
    first_key = jax.random.fold_in(own_key, 0)
    base_rows = jax.random.normal(first_key, (VIEWS, FRAME_COUNT, D), jnp.float32)
    return jnp.clip(base_rows, -4.0, 4.0).astype(jnp.bfloat16)


def draw_head_proj(key, part):
    own_key = jax.random.fold_in(key, 47)
    first_key = jax.random.fold_in(own_key, 0)
    columns = jax.random.normal(first_key, (D, AHEADS, 3, AHD), jnp.float32) / math.sqrt(D)
    return jnp.clip(columns, -8.0, 8.0).reshape(D, AHEADS * 3 * AHD).astype(jnp.bfloat16)


def level_of(rng, extent, cuts, smallest, top_value):
    def one(position, shards_of):
        draws = jax.random.uniform(jax.random.fold_in(jax.random.fold_in(rng, 6), position), (shards_of,), jnp.float32, smallest / len(cuts), top_value / len(cuts))
        return jnp.repeat(jnp.exp(draws), extent[position] // shards_of).reshape((-1,) + (1,) * (len(extent) - position - 1))

    loudness = one(*cuts[0])
    for cut in cuts[1:]:
        loudness = loudness * one(*cut)
    return loudness


def bell_draw(key, dims, spread, limit, cuts=(), dtype=jnp.bfloat16):
    values = spread * jax.random.normal(key, dims, jnp.float32)
    if cuts:
        values = values * level_of(key, dims, cuts, -0.22, 0.18)
    return jnp.clip(values, -limit, limit).astype(dtype)


def setup_inputs(seed: int = 0) -> dict:
    keys = jax.random.split(jax.random.key(seed), 14)
    return {
        "hidden_in": draw_hidden_in(jax.random.fold_in(keys[13], 71), 0),
        "ssm_input": bell_draw(keys[1], (VIEWS, FRAME_COUNT, INNER), 1.0, 6.0, ((0, 2), (1, 16))),
        "gate_input": bell_draw(keys[2], (VIEWS, FRAME_COUNT, INNER), 1.0, 6.0, ((0, 2), (1, 16))),
        "write_map": bell_draw(keys[3], (VIEWS, FRAME_COUNT, STATE), 1.0, 6.0, ((0, 2), (1, 16))),
        "read_map": bell_draw(keys[4], (VIEWS, FRAME_COUNT, STATE), 1.0, 6.0, ((0, 2), (1, 16))),
        "step_size": draw_step_size(jax.random.fold_in(keys[13], 71), 0),
        "decay_log": draw_decay_log(jax.random.fold_in(keys[13], 71), 0),
        "skip_gain": jnp.clip(jax.random.uniform(keys[7], (HEADS,), jnp.float32, 0.5, 1.5), 0.5, 1.5),
        "norm_gain": jnp.clip(1.0 + 0.15 * jax.random.normal(keys[8], (INNER,), jnp.float32), 0.25, 1.75),
        "mixer_out": bell_draw(keys[9], (INNER, D), INNER ** -0.5, 0.1875, ((0, 32),)),
        "attn_gain": jnp.clip(1.0 + 0.15 * jax.random.normal(keys[10], (D,), jnp.float32), 0.25, 1.75),
        "head_proj": draw_head_proj(jax.random.fold_in(keys[13], 71), 0),
        "attn_out": bell_draw(keys[12], (AHEADS * AHD, D), (AHEADS * AHD) ** -0.5, 0.25, ((1, 32),)),
    }


small_offset = 1e-05
highest = lax.Precision.HIGHEST

def ssd_block(x_heads, step_block, a_negative, write_block, read_block, carry_state):
    length = x_heads.shape[1]
    write_float = write_block.astype(jnp.float32)
    read_float = read_block.astype(jnp.float32)
    log_decay = step_block * a_negative
    cumulative = jnp.cumsum(log_decay, axis=1)
    positions = jnp.arange(length)
    lower_mask = (positions[:, None] >= positions[None, :])[None, :, :, None]
    between = cumulative[:, :, None, :] - cumulative[:, None, :, :]
    decay_table = jnp.exp(jnp.where(lower_mask, between, -1e+30))
    intersection = jnp.einsum('vin,vjn->vij', read_block, write_block, preferred_element_type=jnp.float32)
    mix_weight = decay_table * intersection[:, :, :, None] * step_block[:, None, :, :]
    result = jnp.einsum('vijh,vjhp->vihp', mix_weight, x_heads, precision=highest)
    result = result + jnp.einsum('vin,vhpn->vihp', read_float, carry_state, precision=highest) * jnp.exp(cumulative)[:, :, :, None]
    tail_weight = jnp.exp(cumulative[:, -1:, :] - cumulative) * step_block
    new_state = jnp.exp(cumulative[:, -1, :])[:, :, None, None] * carry_state
    new_state = new_state + jnp.einsum('vjh,vjn,vjhp->vhpn', tail_weight, write_float, x_heads, precision=highest)
    return (result, new_state)

def gate_norm(ssd_out, input_block, gate_block, skip_gain, norm_gain):
    view_count, length = (input_block.shape[0], input_block.shape[1])
    x_heads = input_block.astype(jnp.float32).reshape(view_count, length, HEADS, HDIM)
    with_skip = ssd_out + skip_gain[:, None] * x_heads
    gated = with_skip.reshape(view_count, length, HEADS * HDIM) * jax.nn.silu(gate_block.astype(jnp.float32))
    inverse_rms = lax.rsqrt(lax.optimization_barrier(jnp.mean(gated * gated, axis=-1, keepdims=True)) + small_offset)
    return (gated * inverse_rms * norm_gain).astype(jnp.bfloat16)

def attend_heads(row_block, weights, attn_gain):
    view_count, frames, feature_width = row_block.shape
    as_float = row_block.astype(jnp.float32)
    normed = (as_float * lax.rsqrt(lax.optimization_barrier(jnp.mean(as_float * as_float, axis=-1, keepdims=True)) + small_offset) * attn_gain).astype(jnp.bfloat16)
    head_count = weights.shape[1] // (3 * AHD)
    projected = jnp.dot(normed.reshape(view_count * frames, feature_width), weights, preferred_element_type=jnp.float32)
    projected = projected.astype(jnp.bfloat16).reshape(view_count, frames, head_count, 3, AHD)
    query_rows = projected[:, :, :, 0].astype(jnp.float32)
    key_rows = projected[:, :, :, 1].astype(jnp.float32)
    value_rows = projected[:, :, :, 2].astype(jnp.float32)
    scores = jnp.einsum('vfep,wfep->fevw', query_rows, key_rows) * AHD ** (-0.5)
    probs = jax.nn.softmax(scores, axis=-1).astype(jnp.bfloat16)
    context = jnp.einsum('fevw,wfep->vfep', probs.astype(jnp.float32), value_rows).astype(jnp.bfloat16)
    return context.reshape(view_count, frames, head_count * AHD)

def reference(hidden_in, ssm_input, gate_input, write_map, read_map, step_size, decay_log, skip_gain, norm_gain, mixer_out, attn_gain, head_proj, attn_out):
    a_negative = -jnp.exp(decay_log)
    block_count = FRAME_COUNT // BLOCK

    def blocked(array):
        return jnp.moveaxis(array.reshape(VIEWS, block_count, BLOCK, array.shape[2]), 1, 0)
    inputs = (blocked(hidden_in), blocked(ssm_input), blocked(gate_input), blocked(write_map), blocked(read_map), blocked(step_size))

    def advance(carry_state, pieces):
        hidden_block, input_block, gate_block, write_block, read_block, step_block = pieces
        x_heads = input_block.astype(jnp.float32).reshape(VIEWS, BLOCK, HEADS, HDIM)
        ssd_out, carry_state = ssd_block(x_heads, step_block, a_negative, write_block, read_block, carry_state)
        mixer = gate_norm(ssd_out, input_block, gate_block, skip_gain, norm_gain)
        projected = jnp.dot(mixer.reshape(VIEWS * BLOCK, INNER), mixer_out, preferred_element_type=jnp.float32)
        residual = (hidden_block.astype(jnp.float32) + projected.reshape(VIEWS, BLOCK, D)).astype(jnp.bfloat16)
        return (carry_state, residual)
    start_state = jnp.zeros((VIEWS, HEADS, HDIM, STATE), jnp.float32)
    final_state, residual = lax.scan(advance, start_state, inputs)

    def attend(residual_block):
        context = attend_heads(residual_block, head_proj, attn_gain)
        update = jnp.dot(context.reshape(VIEWS * BLOCK, AHEADS * AHD), attn_out, preferred_element_type=jnp.float32)
        return (residual_block.astype(jnp.float32) + update.reshape(VIEWS, BLOCK, D)).astype(jnp.bfloat16)
    finished = lax.map(attend, residual)
    return jnp.moveaxis(finished, 0, 1).reshape(VIEWS, FRAME_COUNT, D)
```

```python
import functools
import jax
import jax.numpy as jnp
from jax import lax
from jax.experimental import pallas as pl
from jax.experimental.pallas import tpu as pltpu
from jax.sharding import PartitionSpec as P

HEADS = 16
HDIM = 64
STATE = 128
BLOCK = 128
AHD = 64
GROUP = 4

small_offset = 1e-05
highest = lax.Precision.HIGHEST
f32 = jnp.float32
bf16 = jnp.bfloat16


def entering(part, axis, combine, identity):
    place = lax.axis_index(axis)
    gathered = jax.tree.map(lambda a: lax.all_gather(a, axis), part)
    state = jax.tree.map(lambda a, e: jnp.zeros_like(a) + jnp.asarray(e, a.dtype), part, identity)

    def one(lap, state):
        return combine(
            state, jax.tree.map(lambda a: lax.dynamic_index_in_dim(a, lap, 0, False), gathered)
        )

    return lax.fori_loop(0, place, one, state)


def ssd_block(x_heads, step_block, a_negative, write_block, read_block, carry_state):
    length = x_heads.shape[1]
    x_local = x_heads[0]
    steps_major = step_block[0].T
    read_float = read_block[0].astype(jnp.float32)
    write_float = write_block[0].astype(jnp.float32)
    cumulative = jnp.cumsum(steps_major * a_negative[:, None], axis=1)
    positions = jnp.arange(length)
    lower_mask = (positions[:, None] >= positions[None, :])[None, :, :]
    between = cumulative[:, :, None] - cumulative[:, None, :]
    decay_table = jnp.exp(jnp.where(lower_mask, between, -1e30))
    intersection = jnp.dot(read_block[0], write_block[0].T, preferred_element_type=jnp.float32)
    mix_weight = decay_table * intersection[None, :, :] * steps_major[:, None, :]
    result = jnp.einsum("hij,jhp->ihp", mix_weight, x_local, precision=highest)
    state_now = carry_state[0]
    result = (
        result
        + jnp.einsum("in,hpn->ihp", read_float, state_now, precision=highest)
        * jnp.exp(cumulative).T[:, :, None]
    )
    tail_weight = jnp.exp(cumulative[:, -1:] - cumulative) * steps_major
    new_state = jnp.exp(cumulative[:, -1])[:, None, None] * state_now
    new_state = new_state + jnp.einsum(
        "hj,jn,jhp->hpn", tail_weight, write_float, x_local, precision=highest
    )
    return (result[None], new_state[None])


def gate_norm(ssd_out, input_block, gate_block, skip_gain, norm_gain):
    view_count, length = (input_block.shape[0], input_block.shape[1])
    x_heads = input_block.astype(jnp.float32).reshape(view_count, length, HEADS, HDIM)
    with_skip = ssd_out + skip_gain[:, None] * x_heads
    gated = with_skip.reshape(view_count, length, HEADS * HDIM) * jax.nn.silu(
        gate_block.astype(jnp.float32)
    )
    inverse_rms = lax.rsqrt(jnp.mean(gated * gated, axis=-1, keepdims=True) + small_offset)
    return (gated * inverse_rms * norm_gain).astype(jnp.bfloat16)


def attend_heads(row_block, weights, attn_gain):
    view_count, frames, feature_width = row_block.shape
    as_float = row_block.astype(jnp.float32)
    normed = (
        as_float
        * lax.rsqrt(jnp.mean(as_float * as_float, axis=-1, keepdims=True) + small_offset)
        * attn_gain
    ).astype(jnp.bfloat16)
    head_count = weights.shape[1] // (3 * AHD)
    projected = jnp.dot(
        normed.reshape(view_count * frames, feature_width),
        weights,
        preferred_element_type=jnp.float32,
    )
    projected = projected.astype(jnp.bfloat16).reshape(view_count, frames, head_count, 3, AHD)
    query_rows = projected[:, :, :, 0]
    key_rows = projected[:, :, :, 1]
    value_rows = projected[:, :, :, 2]
    scores = jnp.einsum(
        "vfep,wfep->fevw", query_rows, key_rows, preferred_element_type=jnp.float32
    ) * AHD ** (-0.5)
    probs = jax.nn.softmax(scores, axis=-1).astype(jnp.bfloat16)
    context = jnp.einsum(
        "fevw,wfep->vfep", probs, value_rows, preferred_element_type=jnp.float32
    ).astype(jnp.bfloat16)
    return context.reshape(view_count, frames, head_count * AHD)


def per_device_any(
    hidden_in,
    ssm_input,
    gate_input,
    write_map,
    read_map,
    step_size,
    decay_log,
    skip_gain,
    norm_gain,
    mixer_out,
    attn_gain,
    head_proj,
    attn_out,
):
    length = ssm_input.shape[1]
    block_count = length // BLOCK
    a_negative = -jnp.exp(decay_log)

    def blocked(array):
        return jnp.moveaxis(array.reshape(1, block_count, BLOCK, array.shape[2]), 1, 0)

    def advance(carry_state, pieces):
        input_block, write_block, read_block, step_block = pieces
        x_heads = input_block.astype(jnp.float32).reshape(1, BLOCK, HEADS, HDIM)
        ssd_out, carry_state = ssd_block(
            x_heads, step_block, a_negative, write_block, read_block, carry_state
        )
        return (carry_state, ssd_out)

    start_state = jnp.zeros((1, HEADS, HDIM, STATE), jnp.float32)
    local_state, outputs = lax.scan(
        advance,
        start_state,
        (blocked(ssm_input), blocked(write_map), blocked(read_map), blocked(step_size)),
    )
    local_out = jnp.moveaxis(outputs, 0, 1).reshape(1, length, HEADS, HDIM)
    cumulative = jnp.cumsum(step_size * a_negative, axis=1)
    device_decay = cumulative[:, -1, :]

    def combine(earlier, later):
        return (earlier[0] + later[0], jnp.exp(later[0])[:, :, None, None] * earlier[1] + later[1])

    carried = entering(
        (device_decay, local_state),
        "tm",
        combine,
        (jnp.zeros_like(device_decay), jnp.zeros_like(local_state)),
    )
    incoming = jnp.einsum(
        "vtn,vhpn->vthp", read_map.astype(jnp.float32), carried[1], precision=highest
    )
    ssd_out = local_out + incoming * jnp.exp(cumulative)[:, :, :, None]
    mixer = gate_norm(ssd_out, ssm_input, gate_input, skip_gain, norm_gain)[0]
    projected = jnp.dot(
        mixer,
        lax.all_gather(mixer_out, ("view", "tm"), axis=0, tiled=True),
        preferred_element_type=jnp.float32,
    )
    residual = (hidden_in[0].astype(jnp.float32) + projected).astype(jnp.bfloat16)
    out_weight = lax.all_gather(attn_out, ("view", "tm"), axis=1, tiled=True)
    every_view = lax.all_gather(residual[None], "view", axis=0, tiled=True)
    context = attend_heads(every_view, head_proj, attn_gain)
    own_context = lax.all_to_all(context, "view", split_axis=0, concat_axis=2, tiled=True)
    update = jnp.dot(own_context[0], out_weight, preferred_element_type=jnp.float32)
    result = (residual.astype(jnp.float32) + update).astype(jnp.bfloat16)[None]
    return result


def spread(heads):
    row = lax.broadcasted_iota(jnp.int32, (heads, heads * HDIM), 0)
    col = lax.broadcasted_iota(jnp.int32, (heads, heads * HDIM), 1)
    return (col // HDIM == row).astype(f32)


def three_parts(v):
    hi = v.astype(bf16)
    rest = v - hi.astype(f32)
    mid = rest.astype(bf16)
    low = (rest - mid.astype(f32)).astype(bf16)
    return hi, mid, low


def decay_rows(total):
    hi, mid, low = three_parts(total)
    row = lax.broadcasted_iota(jnp.int32, (16, total.shape[1]), 0)
    tile = jnp.where(row == 0, hi.astype(f32), 0.0)
    tile = jnp.where(row == 1, mid.astype(f32), tile)
    tile = jnp.where(row == 2, low.astype(f32), tile)
    return tile.astype(bf16)


def read_decay(tile):
    return jnp.sum(tile.astype(f32), axis=0, keepdims=True)


def running_sum(step, decay_log):
    length = step.shape[0]
    log_decay = step * -jnp.exp(decay_log)
    row = lax.broadcasted_iota(jnp.int32, (length, length), 0)
    col = lax.broadcasted_iota(jnp.int32, (length, length), 1)
    lower = (row >= col).astype(f32)
    return jnp.dot(lower, log_decay, precision=highest, preferred_element_type=f32)


def state_kernel(place_ref, x_ref, write_ref, step_ref, decay_ref, o0, o1, o2, o3, scr):
    mine = place_ref[0]
    step = step_ref[...]
    cum = running_sum(step, decay_ref[...])
    end = cum[-1:, :]
    table = spread(HEADS)
    tail = jnp.dot(jnp.exp(end - cum) * step, table, precision=highest, preferred_element_type=f32)
    total = jnp.dot(end, table, precision=highest, preferred_element_type=f32)
    weighted = (x_ref[...].astype(f32) * tail).astype(bf16)
    state = lax.dot_general(
        write_ref[...], weighted, (((0,), (0,)), ((), ())), preferred_element_type=f32
    )
    width = state.shape[1] // GROUP
    rows = decay_rows(total)
    for q in range(GROUP):
        scr[q, :STATE, :] = state[:, q * width : (q + 1) * width].astype(bf16)
        scr[q, STATE:, :] = rows[:, q * width : (q + 1) * width]
    for j, o in enumerate((o0, o1, o2, o3)):
        o[...] = scr[mine ^ j]


def plane_kernel(place_ref, s0, s1, s2, s3, o, scr):
    mine = place_ref[0]
    for j, s in enumerate((s0, s1, s2, s3)):
        scr[mine ^ j] = s[...]
    total = None
    acc = None
    for q in range(GROUP):
        decay = read_decay(scr[q, STATE:, :])
        state = scr[q, :STATE, :].astype(f32)
        acc = state if acc is None else acc * jnp.exp(decay) + state
        total = decay if total is None else total + decay
    o[:STATE, :] = acc.astype(bf16)
    o[STATE:, :] = decay_rows(total)


def enter_kernel(place_ref, s0, s1, s2, s3, t1, t2, t3, o0, o1, o2, o3, scr, out):
    mine = place_ref[0]
    for j, s in enumerate((s0, s1, s2, s3)):
        scr[mine ^ j] = s[...]
    acc = t3[:STATE, :].astype(f32)
    for t in (t2, t1):
        acc = acc * jnp.exp(read_decay(t[STATE:, :])) + t[:STATE, :].astype(f32)
    for q in range(GROUP):
        out[q] = acc.astype(bf16)
        if q + 1 < GROUP:
            decay = read_decay(scr[q, STATE:, :])
            acc = acc * jnp.exp(decay) + scr[q, :STATE, :].astype(f32)
    for j, o in enumerate((o0, o1, o2, o3)):
        o[...] = out[mine ^ j]


def local_kernel(
    x_ref, gate_ref, write_ref, read_ref, step_ref, step_t_ref, decay_ref, decay_t_ref, skip_ref,
    g1_ref, g2_ref,
):
    length = x_ref.shape[0]
    half = length // 2
    step = step_ref[...]
    cum = running_sum(step, decay_ref[...])
    step_t = step_t_ref[...]
    log_t = step_t * -jnp.exp(decay_t_ref[...])
    row = lax.broadcasted_iota(jnp.int32, (length, length), 0)
    col = lax.broadcasted_iota(jnp.int32, (length, length), 1)
    upper = (row <= col).astype(f32)
    cum_t = jnp.dot(log_t, upper, precision=highest, preferred_element_type=f32)
    table = spread(HEADS)
    inter = lax.dot_general(
        read_ref[...], write_ref[...], (((1,), (1,)), ((), ())), preferred_element_type=f32
    )
    grow = jnp.dot(jnp.exp(cum), table, precision=highest, preferred_element_type=f32)
    skip = jnp.dot(skip_ref[...], table, precision=highest, preferred_element_type=f32)
    lane = lax.broadcasted_iota(jnp.int32, (length, 2 * HDIM), 1)
    for top, rows, cols in ((0, half, half), (half, half, length)):
        keep = (
            lax.broadcasted_iota(jnp.int32, (rows, cols), 0) + top
            >= lax.broadcasted_iota(jnp.int32, (rows, cols), 1)
        )
        near = inter[top : top + rows, :cols]
        for pair in range(HEADS // 2):
            at = pair * 2 * HDIM
            x_pair = x_ref[:cols, at : at + 2 * HDIM]
            out = None
            for k in range(2):
                h = 2 * pair + k
                between = cum[top : top + rows, h : h + 1] - cum_t[h : h + 1, :cols]
                table_h = jnp.exp(jnp.where(keep, between, -1e30))
                mix = (table_h * near * step_t[h : h + 1, :cols]).astype(bf16)
                own = lane[:cols] < HDIM if k == 0 else lane[:cols] >= HDIM
                part = jnp.dot(
                    mix, jnp.where(own, x_pair, jnp.zeros_like(x_pair)), preferred_element_type=f32
                )
                out = part if out is None else out + part
            here = (slice(top, top + rows), slice(at, at + 2 * HDIM))
            u = gate_ref[here].astype(f32)
            silu = u / (1.0 + jnp.exp(-u))
            x_here = x_ref[here].astype(f32)
            g1_ref[here] = (out + skip[:, at : at + 2 * HDIM] * x_here) * silu
            g2_ref[here] = silu * grow[here]


def place_rows(pieces, dest, place_ref, sem, rows):
    x, z, y, c = (place_ref[i] for i in range(4))
    copies = []
    for i, piece in enumerate(pieces):
        dx, dc = i % 2, i // 2
        for dy in range(2):
            for k, off in enumerate((0, 3, 1, 2)):
                block = dy * 4 + k
                owner = (x ^ dx) * 16 + ((z + off) % 4) * 4 + (y ^ dy) * 2 + (c ^ dc)
                copies.append(
                    pltpu.make_async_copy(
                        piece.at[pl.ds(block * rows, rows), :],
                        dest.at[pl.ds(pl.multiple_of(owner * rows, rows), rows), :],
                        sem.at[i * 8 + block],
                    )
                )
    return copies


def mixer_kernel(
    place_ref, g1_ref, g2_ref, read_ref, e0, e1, e2, e3, hidden_ref, gain_ref, w0, w1, w2, w3,
    o_ref, scr, weight, sem,
):
    copies = place_rows((w0, w1, w2, w3), weight, place_ref, sem, 32)
    for copy in copies:
        copy.start()
    mine = place_ref[2] * 2 + place_ref[3]
    for j, e in enumerate((e0, e1, e2, e3)):
        scr[mine ^ j] = e[...]
    width = e0.shape[1]
    parts = []
    square = None
    for q in range(GROUP):
        here = (slice(None), slice(q * width, (q + 1) * width))
        incoming = jnp.dot(read_ref[...], scr[q], preferred_element_type=f32)
        gated = g1_ref[here] + g2_ref[here] * incoming
        parts.append(gated)
        part = jnp.sum(gated * gated, axis=1, keepdims=True)
        square = part if square is None else square + part
    inverse = lax.rsqrt(square * (1.0 / (GROUP * width)) + small_offset)
    mixer = jnp.concatenate(
        [
            (g * inverse * gain_ref[:, q * width : (q + 1) * width]).astype(bf16)
            for q, g in enumerate(parts)
        ],
        axis=1,
    )
    for copy in copies:
        copy.wait()
    projected = jnp.dot(mixer, weight[...], preferred_element_type=f32)
    o_ref[...] = (hidden_ref[...].astype(f32) + projected).astype(bf16)


def project(rows, gain, weight):
    rows = rows.astype(f32)
    mean = jnp.mean(rows * rows, axis=1, keepdims=True)
    normed = (rows * lax.rsqrt(mean + small_offset) * gain).astype(bf16)
    return jnp.dot(normed, weight, preferred_element_type=f32).astype(bf16)


def split_heads(projected):
    rows = projected.shape[0]
    low = lax.broadcasted_iota(jnp.int32, (rows, 2 * AHD), 1) < AHD
    q, k, v = [], [], []
    for pair in range(projected.shape[1] // (6 * AHD)):
        a, b, c = (
            projected[:, (3 * pair + i) * 2 * AHD : (3 * pair + i + 1) * 2 * AHD].astype(f32)
            for i in range(3)
        )
        q.append(jnp.where(low, a, b))
        k.append(pltpu.roll(jnp.where(low, c, a), AHD, 1))
        v.append(jnp.where(low, b, c))
    return tuple(jnp.concatenate(p, axis=1) for p in (q, k, v))


def project_kernel(rows_ref, gain_ref, weight_ref, o_ref):
    o_ref[...] = project(rows_ref[...], gain_ref[...], weight_ref[...])


def attend_kernel(own_ref, rows_ref, gain_ref, weight_ref, own_out, other_out):
    other = project(rows_ref[...], gain_ref[...], weight_ref[...])
    views = (split_heads(own_ref[...]), split_heads(other))
    width = own_out.shape[1]
    row = lax.broadcasted_iota(jnp.int32, (width, width), 0)
    col = lax.broadcasted_iota(jnp.int32, (width, width), 1)
    same = (row // AHD == col // AHD).astype(bf16)

    def score(q, k):
        product = q * k
        hi = product.astype(bf16)
        low = (product - hi.astype(f32)).astype(bf16)
        return (
            jnp.dot(hi, same, preferred_element_type=f32)
            + jnp.dot(low, same, preferred_element_type=f32)
        ) * AHD ** (-0.5)

    for i, out in enumerate((own_out, other_out)):
        s = [score(views[i][0], views[j][1]) for j in range(2)]
        top = jnp.maximum(s[0], s[1])
        e = [jnp.exp(v - top) for v in s]
        scale = 1.0 / (e[0] + e[1])
        p = [(v * scale).astype(bf16).astype(f32) for v in e]
        out[...] = (p[0] * views[0][2] + p[1] * views[1][2]).astype(bf16)


def output_kernel(place_ref, residual_ref, mine_ref, other_ref, a0, a1, a2, a3, o_ref, ctx, weight, sem):
    copies = place_rows((a0, a1, a2, a3), weight, place_ref, sem, 32)
    for copy in copies:
        copy.start()
    x = place_ref[0]
    ctx[x] = mine_ref[...]
    ctx[x ^ 1] = other_ref[...]
    for copy in copies:
        copy.wait()
    rows = jnp.concatenate([ctx[0], ctx[1]], axis=1)
    update = lax.dot_general(
        rows, weight[...], (((1,), (1,)), ((), ())), preferred_element_type=f32
    )
    o_ref[...] = (residual_ref[...].astype(f32) + update).astype(bf16)


def vmem():
    return pl.BlockSpec(memory_space=pltpu.VMEM)


def call(kernel, inputs, outs, scratch=(), scalars=0, raw=(), flops=0, name=None):
    specs = []
    for i in range(len(inputs)):
        if i < scalars:
            specs.append(pl.BlockSpec(memory_space=pltpu.SMEM))
        elif i in raw:
            specs.append(pl.BlockSpec(memory_space=pl.ANY))
        else:
            specs.append(vmem())
    moved = sum(a.size * a.dtype.itemsize for a in inputs) + sum(
        o.size * o.dtype.itemsize for o in outs
    )
    result = pl.pallas_call(
        kernel,
        out_shape=tuple(outs),
        in_specs=specs,
        out_specs=tuple(vmem() for _ in outs),
        scratch_shapes=list(scratch),
        cost_estimate=pl.CostEstimate(flops=flops, transcendentals=0, bytes_accessed=moved),
        compiler_params=pltpu.CompilerParams(vmem_limit_bytes=50 * 2**20),
        name=name,
    )(*inputs)
    return result if len(outs) > 1 else result[0]


def shape(dims, dtype):
    return jax.ShapeDtypeStruct(dims, dtype)


def gather_pieces(shard, moves):
    core, across_y, across_x, z_up, z_down, z_two = moves
    parts = [shard] + [lax.ppermute(shard, "tm", m) for m in (z_up, z_down, z_two)]
    lane = jnp.concatenate(parts, axis=0)
    lane = jnp.concatenate([lane, lax.ppermute(lane, "tm", across_y)], axis=0)
    far = lax.ppermute(lane, "view", across_x)
    return (lane, far, lax.ppermute(lane, "tm", core), lax.ppermute(far, "tm", core))


def per_device(
    ranges,
    hidden_in,
    ssm_input,
    gate_input,
    write_map,
    read_map,
    step_size,
    decay_log,
    skip_gain,
    norm_gain,
    mixer_out,
    attn_gain,
    head_proj,
    attn_out,
):
    hidden, x, gate = hidden_in[0], ssm_input[0], gate_input[0]
    write, read, step = write_map[0], read_map[0], step_size[0]
    length, inner = x.shape
    width = inner // GROUP
    view, range_at = lax.axis_index("view"), lax.axis_index("tm")
    mine = (range_at % GROUP).astype(jnp.int32)[None]
    place = jnp.stack(
        [view, range_at // GROUP, range_at // 2 % 2, range_at % 2]
    ).astype(jnp.int32)

    flip = {j: [(i, i ^ j) for i in range(ranges)] for j in range(1, GROUP)}
    along = {j: [(i, (i + GROUP * j) % ranges) for i in range(ranges)] for j in (-1, 1, 2)}
    later = {j: [(i, i + GROUP * j) for i in range(ranges - GROUP * j)] for j in range(1, GROUP)}
    swap = [(0, 1), (1, 0)]
    moves = (flip[1], flip[2], swap, along[1], along[-1], along[2])

    message = shape((STATE + 16, width), bf16)
    scratch = pltpu.VMEM((GROUP, STATE + 16, width), bf16)
    decay_row = decay_log[None]
    states = call(
        state_kernel,
        (mine, x, write, step, decay_row),
        (message,) * GROUP,
        (scratch,),
        scalars=1,
        flops=2 * STATE * length * inner,
        name="state",
    )
    states = (states[0],) + tuple(lax.ppermute(states[j], "tm", flip[j]) for j in range(1, GROUP))
    plane = call(
        plane_kernel, (mine,) + states, (message,), (scratch,), scalars=1, name="plane"
    )
    planes = tuple(lax.ppermute(plane, "tm", later[j]) for j in range(1, GROUP))
    entry = shape((STATE, width), bf16)
    entries = call(
        enter_kernel,
        (mine,) + states + planes,
        (entry,) * GROUP,
        (scratch, pltpu.VMEM((GROUP, STATE, width), bf16)),
        scalars=1,
        name="enter",
    )
    entries = (entries[0],) + tuple(
        lax.ppermute(entries[j], "tm", flip[j]) for j in range(1, GROUP)
    )
    g1, g2 = call(
        local_kernel,
        (x, gate, write, read, step, step.T, decay_row, decay_log[:, None], skip_gain[None]),
        (shape((length, inner), f32),) * 2,
        flops=8 * length * length * inner,
        name="local",
    )
    mixer_pieces = gather_pieces(mixer_out, moves)
    out_pieces = gather_pieces(attn_out.T, moves)
    residual = call(
        mixer_kernel,
        (place, g1, g2, read) + entries + (hidden, norm_gain[None]) + mixer_pieces,
        (shape(hidden.shape, bf16),),
        (
            pltpu.VMEM((GROUP, STATE, width), bf16),
            pltpu.VMEM((inner, hidden.shape[1]), bf16),
            pltpu.SemaphoreType.DMA((32,)),
        ),
        scalars=1,
        raw=range(10, 14),
        flops=2 * length * inner * hidden.shape[1],
        name="mixer",
    )
    other_rows = lax.ppermute(residual, "view", swap)
    gain_row = attn_gain[None]
    own_projected = call(
        project_kernel,
        (residual, gain_row, head_proj),
        (shape((length, head_proj.shape[1]), bf16),),
        flops=2 * length * head_proj.size,
        name="project",
    )
    context = shape((length, head_proj.shape[1] // 3), bf16)
    mine_context, other_context = call(
        attend_kernel,
        (own_projected, other_rows, gain_row, head_proj),
        (context, context),
        flops=2 * length * head_proj.size,
        name="attend",
    )
    other_context = lax.ppermute(other_context, "view", swap)
    result = call(
        output_kernel,
        (place, residual, mine_context, other_context) + out_pieces,
        (shape(residual.shape, bf16),),
        (
            pltpu.VMEM((2,) + context.shape, bf16),
            pltpu.VMEM((hidden.shape[1], attn_out.shape[0]), bf16),
            pltpu.SemaphoreType.DMA((32,)),
        ),
        scalars=1,
        raw=range(4, 8),
        flops=2 * length * attn_out.shape[0] * hidden.shape[1],
        name="output",
    )
    return result[None]


def solution(mesh):
    views, ranges = mesh.shape["view"], mesh.shape["tm"]
    if (views, ranges) == (2, 16):
        body = functools.partial(per_device, ranges)
    else:
        body = per_device_any
    return jax.shard_map(
        body,
        mesh=mesh,
        in_specs=(
            P("view", "tm", None),
            P("view", "tm", None),
            P("view", "tm", None),
            P("view", "tm", None),
            P("view", "tm", None),
            P("view", "tm", None),
            P(),
            P(),
            P(),
            P(("view", "tm"), None),
            P(),
            P(None, "view"),
            P(None, ("view", "tm")),
        ),
        out_specs=P("view", "tm", None),
        check_vma=False,
    )
```
